32 devices in a mesh: dp: 16 (over z, x, core), seq: 2 (over y).
Axes of the slice: x: 2, y: 2, z: 4, core: 2. Of those that a mesh axis runs over, the one named last changes fastest.
Arguments:
- tokens: bfloat16 [16, 1152, 1024], P('dp', 'seq'), may hold values from -6 to 6
- w_qkv: bfloat16 [1024, 3072], P('dp'), may hold values from -0.1875 to 0.1875
- w_out: bfloat16 [1024, 1024], P('dp'), may hold values from -1 to 1
- w_up: bfloat16 [1024, 4096], P('dp'), may hold values from -0.1875 to 0.1875
- w_down: bfloat16 [4096, 1024], P('dp'), may hold values from -0.09375 to 0.09375
- gains: bfloat16 [1024, 2], P('dp'), may hold values from 0.5 to 1.5
- biases: bfloat16 [1024, 6], P('dp'), may hold values from -1.1953125 to 1.1953125
- up_bias: bfloat16 [4096], P('dp'), may hold values from -1.1953125 to 1.1953125
- valid: int32 [16], P('dp'), may hold values from 577 to 1152
- cotangent: bfloat16 [16, 1152, 1024], P('dp', 'seq'), may hold values from -6 to 6
Outputs:
- out_tokens: bfloat16 [16, 1152, 1024], P('dp', 'seq')
- grad_tokens: float32 [16, 1152, 1024], P('dp', 'seq')
- grad_qkv: float32 [1024, 3072], P('dp')
- grad_out: float32 [1024, 1024], P('dp')
- grad_up: float32 [1024, 4096], P('dp')
- grad_down: float32 [4096, 1024], P('dp')
- grad_gains: float32 [1024, 2], P('dp')
- grad_biases: float32 [1024, 6], P('dp')
- grad_up_bias: float32 [4096], P('dp')
The draws below stay inside these ranges and needn't reach their ends.
Inputs may be any that keep to these rules, and one draw needn't show every extreme that they name: valid counts of the images; keys at positions from valid on are padding.
All inputs are finite; a program needn't handle non-finite values.
Results may differ from the reference program's by a relative error of at most 0.019.
Values may be sent and summed in bfloat16 or wider, within the bound.
A program may use at most 256 MiB of HBM per device.

```python
import jax
import jax.numpy as jnp
from jax import lax

D = 1024
FF = 4096
H = 16
SEQ = 1152
HD = 64
IMAGES = 16


def set_ends(drawn, own_key, least, top_value):
    spot = [jax.random.randint(jax.random.fold_in(own_key, axis), (), 0, length) for axis, length in enumerate(drawn.shape)]
    main_axis = drawn.shape.index(max(drawn.shape))
    neighbour = spot[:main_axis] + [(spot[main_axis] + 1) % drawn.shape[main_axis]] + spot[main_axis + 1:]
    return drawn.at[tuple(spot)].set(least).at[tuple(neighbour)].set(top_value)


def shard_levels(key, dims, split, smallest, high):
    def one(axis_at, shards_of):
        draws = jax.random.uniform(jax.random.fold_in(jax.random.fold_in(key, 6), axis_at), (shards_of,), jnp.float32, smallest / len(split), high / len(split))
        return jnp.repeat(jnp.exp(draws), dims[axis_at] // shards_of).reshape((-1,) + (1,) * (len(dims) - axis_at - 1))

    factor_of = one(*split[0])
    for cut in split[1:]:
        factor_of = factor_of * one(*cut)
    return factor_of


def gaussian(stream_key, extent, deviation, bound, split=(), kind=jnp.bfloat16):
    drawn = jax.random.normal(stream_key, extent, jnp.float32) * deviation
    if len(split) > 0:
        drawn = shard_levels(stream_key, extent, split, -0.22, 0.18) * drawn
    return jnp.clip(drawn, min=-bound, max=bound).astype(kind)


def setup_inputs(seed: int = 0) -> dict:
    key_of = jax.random.split(jax.random.key(seed), 11)
    return {
        "tokens": gaussian(key_of[0], (IMAGES, SEQ, D), 1.0, 6.0, ((0, 16), (1, 2))),
        "w_qkv": gaussian(key_of[1], (D, 3 * D), D ** -0.5, 0.1875, ((0, 16),)),
        "w_out": gaussian(key_of[2], (D, D), (D // 32) ** -0.5, 1.0, ((0, 16),)),
        "w_up": gaussian(key_of[3], (D, FF), D ** -0.5, 0.1875, ((0, 16),)),
        "w_down": gaussian(key_of[4], (FF, D), FF ** -0.5, 0.09375, ((0, 16),)),
        "gains": jnp.clip(1.0 + 0.1 * jax.random.normal(key_of[5], (D, 2), jnp.float32), 0.5, 1.5).astype(jnp.bfloat16),
        "biases": gaussian(key_of[6], (D, 6), 0.2, 1.1953125, ((0, 16),)),
        "up_bias": gaussian(key_of[7], (FF,), 0.2, 1.1953125, ((0, 16),)),
        "valid": set_ends(jax.random.randint(key_of[8], (IMAGES,), SEQ // 2 + 1, SEQ + 1), jax.random.fold_in(key_of[8], 1), SEQ // 2 + 1, SEQ).astype(jnp.int32),
        "cotangent": gaussian(key_of[9], (IMAGES, SEQ, D), 1.0, 6.0, ((0, 16), (1, 2))),
    }


EPSILON = 1e-06
NEG_FILL = -1e+30

@jax.custom_vjp
def low(v):
    return lax.optimization_barrier(v.astype(jnp.bfloat16)).astype(jnp.float32)

@jax.custom_vjp
def low_back(v):
    return v

def low_keep(v):
    return (low(v), None)

def low_pass(kept, grad):
    return (grad,)

def back_keep(v):
    return (v, None)

def back_low(kept, grad):
    return (low(grad),)
low.defvjp(low_keep, low_pass)
low_back.defvjp(back_keep, back_low)

def layer_norm(values, scales, offset):
    average = lax.optimization_barrier(jnp.mean(values, axis=-1, keepdims=True))
    centered = values - average
    variance = lax.optimization_barrier(jnp.mean(centered * centered, axis=-1, keepdims=True))
    return centered * lax.rsqrt(variance + EPSILON) * scales + offset

def attend_one(packed):
    queries, keyset, values, length = packed
    scores = jnp.einsum('qhd,khd->hqk', queries, keyset, precision=lax.Precision.HIGHEST) * HD ** (-0.5)
    scores = low_back(scores)
    allowed = jnp.arange(SEQ, dtype=jnp.int32) < length
    scores = jnp.where(allowed[None, None, :], scores, NEG_FILL)
    row_max = lax.optimization_barrier(jnp.max(scores, axis=-1, keepdims=True))
    exp_scores = jnp.exp(scores - row_max)
    probs = exp_scores / lax.optimization_barrier(jnp.sum(exp_scores, axis=-1, keepdims=True))
    return jnp.einsum('hqk,khd->qhd', low(probs), values, precision=lax.Precision.HIGHEST)

def forward(tokens, w_qkv, w_out, w_up, w_down, gains, biases, up_bias, valid):
    highest = lax.Precision.HIGHEST
    first = low(layer_norm(tokens, gains[:, 0], biases[:, 0]))
    mixed = jnp.einsum('isd,de->ise', first, w_qkv, precision=highest)
    queries = low(low_back(mixed[..., :D] + biases[:, 1]))
    keyset = low(low_back(mixed[..., D:2 * D]))
    values = low(low_back(mixed[..., 2 * D:] + biases[:, 2]))
    head_shape = (IMAGES, SEQ, H, HD)
    attended = lax.map(jax.checkpoint(attend_one), (queries.reshape(head_shape), keyset.reshape(head_shape), values.reshape(head_shape), valid))
    attended = low(low_back(attended.reshape(IMAGES, SEQ, D)))
    branch = low_back(jnp.einsum('isd,de->ise', attended, w_out, precision=highest) + biases[:, 3])
    residual = tokens + branch
    second = low(layer_norm(residual, gains[:, 1], biases[:, 4]))
    upward = low_back(jnp.einsum('isd,df->isf', second, w_up, precision=highest) + up_bias)
    activated = low(jax.nn.gelu(upward, approximate=False))
    return residual + jnp.einsum('isf,fd->isd', activated, w_down, precision=highest) + biases[:, 5]

def reference(tokens, w_qkv, w_out, w_up, w_down, gains, biases, up_bias, valid, cotangent):
    floats = tuple((entry_array.astype(jnp.float32) for entry_array in (tokens, w_qkv, w_out, w_up, w_down, gains, biases, up_bias)))

    def wrapped(*inputs):
        return forward(*inputs, valid)
    output, pull_back = jax.vjp(wrapped, *floats)
    grads = pull_back(cotangent.astype(jnp.float32))
    return (output.astype(jnp.bfloat16), grads[0], grads[1], grads[2], grads[3], grads[4], grads[5], grads[6], grads[7])
```

```python
import functools

import jax
import jax.numpy as jnp
from jax import lax
from jax.experimental import pallas as pl
from jax.experimental.pallas import tpu as pltpu
from jax.sharding import PartitionSpec as P

HD = 64
PAIR = 2 * HD
EPSILON = 1e-06
NEG_FILL = -1e30
SMALL = 128
SPLITS = 2


def layer_norm(values, scales, offset):
    average = jnp.mean(values, axis=-1, keepdims=True)
    centered = values - average
    variance = jnp.mean(centered * centered, axis=-1, keepdims=True)
    return centered * lax.rsqrt(variance + EPSILON) * scales + offset


def dot_f32(a, b, dims):
    return lax.dot_general(a, b, (dims, ((), ())), preferred_element_type=jnp.float32)


def head_masks(dtype):
    lane = lax.broadcasted_iota(jnp.int32, (1, PAIR), 1)
    return (lane < HD).astype(dtype), (lane >= HD).astype(dtype)


def allowed_keys(place_ref, valid_ref, length, shards):
    row = lax.broadcasted_iota(jnp.int32, (shards * length, 1), 0)
    position = row + place_ref[0] * length
    position = jnp.where(position >= shards * length, position - shards * length, position)
    return position < valid_ref[pl.program_id(0)]


def stacked(refs):
    return jnp.concatenate([ref[...] for ref in refs], axis=0)


def forward_kernel(shards, place_ref, valid_ref, q_ref, *refs):
    k_refs, v_refs, (out_ref, lse_ref) = refs[:shards], refs[shards : 2 * shards], refs[2 * shards :]
    allowed = allowed_keys(place_ref, valid_ref, q_ref.shape[0], shards)
    keys, values = stacked(k_refs), stacked(v_refs)
    queries = q_ref[...] * jnp.bfloat16(HD**-0.5)
    total = None
    for head, mask in enumerate(head_masks(jnp.bfloat16)):
        scores = dot_f32(keys, queries * mask, ((1,), (1,)))
        scores = jnp.where(allowed, scores, NEG_FILL)
        top = jnp.max(scores, axis=0, keepdims=True)
        weight = jnp.exp(scores - top)
        row_total = jnp.sum(weight, axis=0, keepdims=True)
        part = dot_f32(values * mask, weight.astype(jnp.bfloat16), ((0,), (0,)))
        part = part / row_total
        total = part if total is None else total + part
        lse_ref[0, 0, head : head + 1, :] = top + jnp.log(row_total)
    out_ref[...] = total.T.astype(out_ref.dtype)


def backward_kernel(shards, place_ref, valid_ref, q_ref, *refs):
    k_refs, v_refs, refs = refs[:shards], refs[shards : 2 * shards], refs[2 * shards :]
    lse_ref, da_ref, dq_ref = refs[:3]
    dk_refs, dv_refs = refs[3 : 3 + shards], refs[3 + shards :]
    length = q_ref.shape[0]
    allowed = allowed_keys(place_ref, valid_ref, length, shards)
    keys, values = stacked(k_refs), stacked(v_refs)
    queries = q_ref[...] * jnp.bfloat16(HD**-0.5)
    grads = da_ref[...]
    dq = dk = dv = None
    for head, mask in enumerate(head_masks(jnp.bfloat16)):
        own_q = queries * mask
        own_g = grads * mask
        scores = dot_f32(keys, own_q, ((1,), (1,)))
        scores = jnp.where(allowed, scores, NEG_FILL)
        probs = jnp.exp(scores - lse_ref[0, 0, head : head + 1, :])
        dprobs = dot_f32(values, own_g, ((1,), (1,)))
        delta = jnp.sum(probs * dprobs, axis=0, keepdims=True)
        dscores = (probs * (dprobs - delta)).astype(jnp.bfloat16)
        part_v = dot_f32(probs.astype(jnp.bfloat16), own_g, ((1,), (0,)))
        part_k = dot_f32(dscores, own_q, ((1,), (0,)))
        part_q = dot_f32(keys * mask, dscores, ((0,), (0,)))
        dq = part_q if dq is None else dq + part_q
        dk = part_k if dk is None else dk + part_k
        dv = part_v if dv is None else dv + part_v
    dq_ref[...] = (dq * HD**-0.5).T.astype(dq_ref.dtype)
    for j in range(shards):
        rows = slice(j * length, (j + 1) * length)
        dk_refs[j][...] = dk[rows].astype(dk_refs[j].dtype)
        dv_refs[j][...] = dv[rows].astype(dv_refs[j].dtype)


def attention_specs(length):
    smem = pl.BlockSpec(memory_space=pltpu.SMEM)
    block = pl.BlockSpec((length, PAIR), lambda i, h: (i, h))
    lse = pl.BlockSpec((1, 1, 2, length), lambda i, h: (i, h, 0, 0))
    return smem, block, lse


def attend_forward(images, place, valid, q, keys, values):
    shards = len(keys)
    rows, width = q.shape
    length, pairs = rows // images, width // PAIR
    smem, block, lse = attention_specs(length)
    return pl.pallas_call(
        functools.partial(forward_kernel, shards),
        grid=(images, pairs),
        in_specs=[smem, smem] + [block] * (1 + 2 * shards),
        out_specs=[block, lse],
        out_shape=[
            jax.ShapeDtypeStruct((rows, width), jnp.bfloat16),
            jax.ShapeDtypeStruct((images, pairs, 2, length), jnp.float32),
        ],
        compiler_params=pltpu.CompilerParams(vmem_limit_bytes=40 * 2**20),
        cost_estimate=pl.CostEstimate(
            flops=8 * shards * rows * length * width, bytes_accessed=12 * rows * width,
            transcendentals=shards * rows * length * width // HD,
        ),
    )(place, valid, q, *keys, *values)


def attend_backward(images, place, valid, q, keys, values, lse_in, da):
    shards = len(keys)
    rows, width = q.shape
    length, pairs = rows // images, width // PAIR
    smem, block, lse = attention_specs(length)
    low = jax.ShapeDtypeStruct((rows, width), jnp.bfloat16)
    wide = jax.ShapeDtypeStruct((rows, width), jnp.float32)
    return pl.pallas_call(
        functools.partial(backward_kernel, shards),
        grid=(images, pairs),
        in_specs=[smem, smem] + [block] * (1 + 2 * shards) + [lse, block],
        out_specs=[block] * (1 + 2 * shards),
        out_shape=[low] + 2 * ([wide] + [low] * (shards - 1)),
        compiler_params=pltpu.CompilerParams(vmem_limit_bytes=48 * 2**20),
        cost_estimate=pl.CostEstimate(
            flops=20 * shards * rows * length * width, bytes_accessed=26 * rows * width,
            transcendentals=shards * rows * length * width // HD,
        ),
    )(place, valid, q, *keys, *values, lse_in, da)


def shift(values, shards, step):
    return lax.ppermute(values, "seq", [(i, (i + step) % shards) for i in range(shards)])


def per_device(tokens, w_qkv, w_out, w_up, w_down, gains, biases, up_bias, valid, cotangent):
    images, local_len, width = tokens.shape
    shard_rows = w_qkv.shape[0]
    ups = up_bias.shape[0] // shard_rows
    hidden = w_up.shape[1]
    token_shape = tokens.shape
    shards = lax.axis_size("seq")
    place = lax.axis_index("seq").astype(jnp.int32).reshape(1)

    gather = functools.partial(lax.all_gather, axis_name="dp", axis=0, tiled=True)
    scatter = functools.partial(
        lax.psum_scatter, axis_name="dp", scatter_dimension=0, tiled=True
    )
    smalls = jnp.concatenate([gains, biases, up_bias.reshape(shard_rows, ups)], axis=1)
    smalls = jnp.pad(smalls, ((0, 0), (0, SMALL - smalls.shape[1])))
    full_qkvs = gather(jnp.concatenate([w_qkv, smalls], axis=1))
    out_up = jnp.concatenate([w_out, w_up], axis=1)
    out_up, full_qkvs = lax.optimization_barrier((out_up, full_qkvs))
    full_out_up = gather(out_up)
    w_down, full_out_up = lax.optimization_barrier((w_down, full_out_up))
    full_down = gather(w_down)

    full_qkv = full_qkvs[:, : 3 * width]
    small = full_qkvs[:, 3 * width :].astype(jnp.float32).T
    gain_one, gain_two = small[0], small[1]
    bias_one, bias_q, bias_v, bias_out, bias_two, bias_down = (small[2 + i] for i in range(6))
    bias_up = small[8 : 8 + ups].T.reshape(-1)
    full_out = full_out_up[:, :width]
    full_up = full_out_up[:, width:]

    flat_tokens = tokens.reshape(-1, width).astype(jnp.float32)
    normed_one, pull_one = jax.vjp(layer_norm, flat_tokens, gain_one, bias_one)
    first = normed_one.astype(jnp.bfloat16)

    piece = width // SPLITS
    groups = []
    for g in range(SPLITS):
        lo, hi = g * piece, (g + 1) * piece
        k = jnp.dot(
            first, full_qkv[:, width + lo : width + hi], preferred_element_type=jnp.float32
        ).astype(jnp.bfloat16)
        v = jnp.dot(
            first, full_qkv[:, 2 * width + lo : 2 * width + hi],
            preferred_element_type=jnp.float32,
        )
        v = (v + bias_v[lo:hi]).astype(jnp.bfloat16)
        q = jnp.dot(first, full_qkv[:, lo:hi], preferred_element_type=jnp.float32)
        q = (q + bias_q[lo:hi]).astype(jnp.bfloat16)
        keys = [k] + [shift(k, shards, -j) for j in range(1, shards)]
        values = [v] + [shift(v, shards, -j) for j in range(1, shards)]
        groups.append((q, keys, values))
    parts = [attend_forward(images, place, valid, *group) for group in groups]
    merged = jnp.concatenate([part[0] for part in parts], axis=1)

    branch = jnp.dot(merged, full_out, preferred_element_type=jnp.float32) + bias_out
    residual = flat_tokens + branch
    normed_two, pull_two = jax.vjp(layer_norm, residual, gain_two, bias_two)
    second = normed_two.astype(jnp.bfloat16)
    upward = jnp.dot(second, full_up, preferred_element_type=jnp.float32) + bias_up
    cdf = 0.5 * (1.0 + lax.erf(upward * 0.5**0.5))
    activated = (upward * cdf).astype(jnp.bfloat16)
    slope = cdf + upward * (jnp.exp(-0.5 * upward * upward) * 0.3989422804014327)
    slope = slope.astype(jnp.bfloat16)

    grad_output = cotangent.reshape(-1, width)
    grad_down = dot_f32(activated, grad_output, ((0,), (0,))).astype(jnp.bfloat16)
    grad_down, full_down, activated = lax.optimization_barrier((grad_down, full_down, activated))
    piece_down = scatter(grad_down)

    grad_act = dot_f32(grad_output, full_down, ((1,), (1,)))
    grad_upward = (grad_act * slope.astype(jnp.float32)).astype(jnp.bfloat16)
    grad_second = dot_f32(grad_upward, full_up, ((1,), (1,)))
    grad_resid_norm, grad_gain_two, grad_bias_two = pull_two(grad_second)
    grad_resid = grad_output.astype(jnp.float32) + grad_resid_norm
    grad_branch = grad_resid.astype(jnp.bfloat16)
    grad_merged = dot_f32(grad_branch, full_out, ((1,), (1,))).astype(jnp.bfloat16)
    grad_up = dot_f32(second, grad_upward, ((0,), (0,))).astype(jnp.bfloat16)
    grad_out_weight = dot_f32(merged, grad_branch, ((0,), (0,))).astype(jnp.bfloat16)
    grad_out_up = jnp.concatenate([grad_out_weight, grad_up], axis=1)
    grad_out_up, grad_merged = lax.optimization_barrier((grad_out_up, grad_merged))
    piece_out_up = scatter(grad_out_up)

    backs = []
    for g, (group, part) in enumerate(zip(groups, parts)):
        lo, hi = g * piece, (g + 1) * piece
        grads = grad_merged[:, lo:hi]
        if g == SPLITS - 1:
            grads, piece_down = lax.optimization_barrier((grads, piece_down))
        dq, *rest = attend_backward(images, place, valid, *group, part[1], grads)
        dk, dv = rest[0], rest[shards]
        for j in range(1, shards):
            dk = dk + shift(rest[j], shards, j).astype(jnp.float32)
            dv = dv + shift(rest[shards + j], shards, j).astype(jnp.float32)
        dk, dv = dk.astype(jnp.bfloat16), dv.astype(jnp.bfloat16)
        backs.append((dq, dk, dv))
    grad_mixed = jnp.concatenate(
        [back[part] for part in range(3) for back in backs], axis=1
    )
    grad_qkv = dot_f32(first, grad_mixed, ((0,), (0,))).astype(jnp.bfloat16)
    grad_first = dot_f32(grad_mixed, full_qkv, ((1,), (1,)))
    grad_tok_norm, grad_gain_one, grad_bias_one = pull_one(grad_first)
    grad_tokens = (grad_resid + grad_tok_norm).reshape(token_shape)

    def token_sum(values):
        return jnp.sum(values.astype(jnp.float32), axis=0)

    small_grads = jnp.stack(
        [
            grad_gain_one, grad_gain_two, grad_bias_one,
            token_sum(grad_mixed[:, :width]), token_sum(grad_mixed[:, 2 * width :]),
            token_sum(grad_branch), grad_bias_two, token_sum(grad_output),
        ],
        axis=1,
    )
    small_grads = jnp.concatenate([small_grads, token_sum(grad_upward).reshape(width, -1)], axis=1)
    small_grads = jnp.pad(small_grads, ((0, 0), (0, SMALL - small_grads.shape[1])))
    grad_qkvs = jnp.concatenate([grad_qkv, small_grads.astype(jnp.bfloat16)], axis=1)
    grad_qkvs, piece_out_up = lax.optimization_barrier((grad_qkvs, piece_out_up))
    piece_qkvs = scatter(grad_qkvs)

    output = residual + jnp.dot(activated, full_down, preferred_element_type=jnp.float32)
    out_tokens = (output + bias_down).astype(jnp.bfloat16).reshape(token_shape)

    def both(values):
        if shards == 2:
            return values.astype(jnp.float32) + shift(values, shards, 1).astype(jnp.float32)
        return lax.psum(values, "seq").astype(jnp.float32)

    total_down, total_out_up, total_qkvs = both(piece_down), both(piece_out_up), both(piece_qkvs)
    total_small = total_qkvs[:, 3 * width :]
    return (
        out_tokens,
        grad_tokens,
        total_qkvs[:, : 3 * width],
        total_out_up[:, :width],
        total_out_up[:, width:],
        total_down,
        total_small[:, :2],
        total_small[:, 2:8],
        total_small[:, 8 : 8 + ups].reshape(-1),
    )


def solution(mesh):
    return jax.shard_map(
        per_device,
        mesh=mesh,
        in_specs=(
            P("dp", "seq", None),
            P("dp", None),
            P("dp", None),
            P("dp", None),
            P("dp", None),
            P("dp", None),
            P("dp", None),
            P("dp"),
            P("dp"),
            P("dp", "seq", None),
        ),
        out_specs=(
            P("dp", "seq", None),
            P("dp", "seq", None),
            P("dp", None),
            P("dp", None),
            P("dp", None),
            P("dp", None),
            P("dp", None),
            P("dp", None),
            P("dp"),
        ),
        check_vma=False,
    )
```

```python
import functools

import jax
import jax.numpy as jnp
from jax import lax
from jax.experimental import pallas as pl
from jax.experimental.pallas import tpu as pltpu
from jax.sharding import PartitionSpec as P

HD = 64
PAIR = 2 * HD
EPSILON = 1e-06
NEG_FILL = -1e30
SMALL = 128
SPLITS = 2


def layer_norm(values, scales, offset):
    average = jnp.mean(values, axis=-1, keepdims=True)
    centered = values - average
    variance = jnp.mean(centered * centered, axis=-1, keepdims=True)
    return centered * lax.rsqrt(variance + EPSILON) * scales + offset


def dot_f32(a, b, dims):
    return lax.dot_general(a, b, (dims, ((), ())), preferred_element_type=jnp.float32)


def head_masks(dtype):
    lane = lax.broadcasted_iota(jnp.int32, (1, PAIR), 1)
    return (lane < HD).astype(dtype), (lane >= HD).astype(dtype)


def allowed_keys(place_ref, valid_ref, length, shards):
    row = lax.broadcasted_iota(jnp.int32, (shards * length, 1), 0)
    position = row + place_ref[0] * length
    position = jnp.where(position >= shards * length, position - shards * length, position)
    return position < valid_ref[pl.program_id(0)]


def stacked(refs):
    return jnp.concatenate([ref[...] for ref in refs], axis=0)


def forward_kernel(shards, place_ref, valid_ref, q_ref, *refs):
    k_refs, v_refs, (out_ref, lse_ref) = refs[:shards], refs[shards : 2 * shards], refs[2 * shards :]
    allowed = allowed_keys(place_ref, valid_ref, q_ref.shape[0], shards)
    keys, values = stacked(k_refs), stacked(v_refs)
    queries = q_ref[...] * jnp.bfloat16(HD**-0.5)
    total = None
    for head, mask in enumerate(head_masks(jnp.bfloat16)):
        scores = dot_f32(keys, queries * mask, ((1,), (1,)))
        scores = jnp.where(allowed, scores, NEG_FILL)
        top = jnp.max(scores, axis=0, keepdims=True)
        weight = jnp.exp(scores - top)
        row_total = jnp.sum(weight, axis=0, keepdims=True)
        part = dot_f32(values * mask, weight.astype(jnp.bfloat16), ((0,), (0,)))
        part = part / row_total
        total = part if total is None else total + part
        lse_ref[0, 0, head : head + 1, :] = top + jnp.log(row_total)
    out_ref[...] = total.T.astype(out_ref.dtype)


def backward_kernel(shards, place_ref, valid_ref, q_ref, *refs):
    k_refs, v_refs, refs = refs[:shards], refs[shards : 2 * shards], refs[2 * shards :]
    lse_ref, da_ref, dq_ref = refs[:3]
    dk_refs, dv_refs = refs[3 : 3 + shards], refs[3 + shards :]
    length = q_ref.shape[0]
    allowed = allowed_keys(place_ref, valid_ref, length, shards)
    keys, values = stacked(k_refs), stacked(v_refs)
    queries = q_ref[...] * jnp.bfloat16(HD**-0.5)
    grads = da_ref[...]
    dq = dk = dv = None
    for head, mask in enumerate(head_masks(jnp.bfloat16)):
        own_q = queries * mask
        own_g = grads * mask
        scores = dot_f32(keys, own_q, ((1,), (1,)))
        scores = jnp.where(allowed, scores, NEG_FILL)
        probs = jnp.exp(scores - lse_ref[0, 0, head : head + 1, :])
        dprobs = dot_f32(values, own_g, ((1,), (1,)))
        delta = jnp.sum(probs * dprobs, axis=0, keepdims=True)
        dscores = (probs * (dprobs - delta)).astype(jnp.bfloat16)
        part_v = dot_f32(probs.astype(jnp.bfloat16), own_g, ((1,), (0,)))
        part_k = dot_f32(dscores, own_q, ((1,), (0,)))
        part_q = dot_f32(keys * mask, dscores, ((0,), (0,)))
        dq = part_q if dq is None else dq + part_q
        dk = part_k if dk is None else dk + part_k
        dv = part_v if dv is None else dv + part_v
    dq_ref[...] = (dq * HD**-0.5).T.astype(dq_ref.dtype)
    for j in range(shards):
        rows = slice(j * length, (j + 1) * length)
        dk_refs[j][...] = dk[rows].astype(dk_refs[j].dtype)
        dv_refs[j][...] = dv[rows].astype(dv_refs[j].dtype)


def attention_specs(length):
    smem = pl.BlockSpec(memory_space=pltpu.SMEM)
    block = pl.BlockSpec((length, PAIR), lambda i, h: (i, h))
    lse = pl.BlockSpec((1, 1, 2, length), lambda i, h: (i, h, 0, 0))
    return smem, block, lse


def attend_forward(images, place, valid, q, keys, values):
    shards = len(keys)
    rows, width = q.shape
    length, pairs = rows // images, width // PAIR
    smem, block, lse = attention_specs(length)
    return pl.pallas_call(
        functools.partial(forward_kernel, shards),
        grid=(images, pairs),
        in_specs=[smem, smem] + [block] * (1 + 2 * shards),
        out_specs=[block, lse],
        out_shape=[
            jax.ShapeDtypeStruct((rows, width), jnp.bfloat16),
            jax.ShapeDtypeStruct((images, pairs, 2, length), jnp.float32),
        ],
        compiler_params=pltpu.CompilerParams(vmem_limit_bytes=40 * 2**20),
        cost_estimate=pl.CostEstimate(
            flops=8 * shards * rows * length * width, bytes_accessed=12 * rows * width,
            transcendentals=shards * rows * length * width // HD,
        ),
    )(place, valid, q, *keys, *values)


def attend_backward(images, place, valid, q, keys, values, lse_in, da):
    shards = len(keys)
    rows, width = q.shape
    length, pairs = rows // images, width // PAIR
    smem, block, lse = attention_specs(length)
    low = jax.ShapeDtypeStruct((rows, width), jnp.bfloat16)
    wide = jax.ShapeDtypeStruct((rows, width), jnp.float32)
    return pl.pallas_call(
        functools.partial(backward_kernel, shards),
        grid=(images, pairs),
        in_specs=[smem, smem] + [block] * (1 + 2 * shards) + [lse, block],
        out_specs=[block] * (1 + 2 * shards),
        out_shape=[low] + 2 * ([wide] + [low] * (shards - 1)),
        compiler_params=pltpu.CompilerParams(vmem_limit_bytes=48 * 2**20),
        cost_estimate=pl.CostEstimate(
            flops=20 * shards * rows * length * width, bytes_accessed=26 * rows * width,
            transcendentals=shards * rows * length * width // HD,
        ),
    )(place, valid, q, *keys, *values, lse_in, da)


def shift(values, shards, step):
    return lax.ppermute(values, "seq", [(i, (i + step) % shards) for i in range(shards)])


def exchange(values, size, bit):
    return lax.ppermute(values, "dp", [(i, i ^ bit) for i in range(size)])


def my_bit(bit):
    return (lax.axis_index("dp") // bit) % 2


def doubling_step(blocks, size, bit):
    other = exchange(blocks, size, bit)
    mine = jnp.stack([blocks, other], axis=1)
    swapped = jnp.stack([other, blocks], axis=1)
    both = jnp.where(my_bit(bit) == 1, swapped, mine)
    return both.reshape((-1,) + blocks.shape[1:])


def halving_step(blocks, size, bit):
    halves = blocks.reshape((-1, 2) + blocks.shape[1:])
    keep = lax.dynamic_index_in_dim(halves, my_bit(bit), 1, keepdims=False)
    send = lax.dynamic_index_in_dim(halves, 1 - my_bit(bit), 1, keepdims=False)
    other = exchange(send, size, bit)
    return (keep.astype(jnp.float32) + other.astype(jnp.float32)).astype(jnp.bfloat16)


def per_device(tokens, w_qkv, w_out, w_up, w_down, gains, biases, up_bias, valid, cotangent):
    images, local_len, width = tokens.shape
    shard_rows = w_qkv.shape[0]
    ups = up_bias.shape[0] // shard_rows
    hidden = w_up.shape[1]
    token_shape = tokens.shape
    shards = lax.axis_size("seq")
    place = lax.axis_index("seq").astype(jnp.int32).reshape(1)

    gather = functools.partial(lax.all_gather, axis_name="dp", axis=0, tiled=True)
    scatter = functools.partial(
        lax.psum_scatter, axis_name="dp", scatter_dimension=0, tiled=True
    )
    smalls = jnp.concatenate([gains, biases, up_bias.reshape(shard_rows, ups)], axis=1)
    smalls = jnp.pad(smalls, ((0, 0), (0, SMALL - smalls.shape[1])))
    full_qkvs = gather(jnp.concatenate([w_qkv, smalls], axis=1))
    out_up = jnp.concatenate([w_out, w_up], axis=1)
    size = lax.axis_size("dp")
    bits = [2**j for j in range(size.bit_length() - 1)]
    blocks_down = w_down[None]
    for bit in reversed(bits[2:]):
        blocks_down = doubling_step(blocks_down, size, bit)
    out_up, full_qkvs, blocks_down = lax.optimization_barrier((out_up, full_qkvs, blocks_down))
    full_out_up = gather(out_up)
    for bit in bits[1:2]:
        blocks_down = doubling_step(blocks_down, size, bit)

    full_qkv = full_qkvs[:, : 3 * width]
    small = full_qkvs[:, 3 * width :].astype(jnp.float32).T
    gain_one, gain_two = small[0], small[1]
    bias_one, bias_q, bias_v, bias_out, bias_two, bias_down = (small[2 + i] for i in range(6))
    bias_up = small[8 : 8 + ups].T.reshape(-1)
    full_out = full_out_up[:, :width]
    full_up = full_out_up[:, width:]

    flat_tokens = tokens.reshape(-1, width).astype(jnp.float32)
    normed_one, pull_one = jax.vjp(layer_norm, flat_tokens, gain_one, bias_one)
    first = normed_one.astype(jnp.bfloat16)

    piece = width // SPLITS
    groups = []
    for g in range(SPLITS):
        lo, hi = g * piece, (g + 1) * piece
        k = jnp.dot(
            first, full_qkv[:, width + lo : width + hi], preferred_element_type=jnp.float32
        ).astype(jnp.bfloat16)
        v = jnp.dot(
            first, full_qkv[:, 2 * width + lo : 2 * width + hi],
            preferred_element_type=jnp.float32,
        )
        v = (v + bias_v[lo:hi]).astype(jnp.bfloat16)
        q = jnp.dot(first, full_qkv[:, lo:hi], preferred_element_type=jnp.float32)
        q = (q + bias_q[lo:hi]).astype(jnp.bfloat16)
        keys = [k] + [shift(k, shards, -j) for j in range(1, shards)]
        values = [v] + [shift(v, shards, -j) for j in range(1, shards)]
        groups.append((q, keys, values))
    parts = [attend_forward(images, place, valid, *group) for group in groups]
    lead, blocks_down = lax.optimization_barrier((parts[0][0], blocks_down))
    for bit in bits[:1]:
        blocks_down = doubling_step(blocks_down, size, bit)
    full_down = blocks_down.reshape(-1, width)
    merged = jnp.concatenate([lead] + [part[0] for part in parts[1:]], axis=1)
    merged, full_down = lax.optimization_barrier((merged, full_down))

    branch = jnp.dot(merged, full_out, preferred_element_type=jnp.float32) + bias_out
    residual = flat_tokens + branch
    normed_two, pull_two = jax.vjp(layer_norm, residual, gain_two, bias_two)
    second = normed_two.astype(jnp.bfloat16)
    upward = jnp.dot(second, full_up, preferred_element_type=jnp.float32) + bias_up
    cdf = 0.5 * (1.0 + lax.erf(upward * 0.5**0.5))
    activated = (upward * cdf).astype(jnp.bfloat16)
    slope = cdf + upward * (jnp.exp(-0.5 * upward * upward) * 0.3989422804014327)
    slope = slope.astype(jnp.bfloat16)

    grad_output = cotangent.reshape(-1, width)
    grad_down = dot_f32(activated, grad_output, ((0,), (0,))).astype(jnp.bfloat16)
    grad_down, full_down, activated = lax.optimization_barrier((grad_down, full_down, activated))
    blocks_down = grad_down.reshape((size,) + w_down.shape)
    for bit in bits[:1]:
        blocks_down = halving_step(blocks_down, size, bit)

    grad_act = dot_f32(grad_output, full_down, ((1,), (1,)))
    grad_upward = (grad_act * slope.astype(jnp.float32)).astype(jnp.bfloat16)
    grad_second = dot_f32(grad_upward, full_up, ((1,), (1,)))
    grad_resid_norm, grad_gain_two, grad_bias_two = pull_two(grad_second)
    grad_resid = grad_output.astype(jnp.float32) + grad_resid_norm
    grad_branch = grad_resid.astype(jnp.bfloat16)
    grad_merged = dot_f32(grad_branch, full_out, ((1,), (1,))).astype(jnp.bfloat16)
    grad_up = dot_f32(second, grad_upward, ((0,), (0,))).astype(jnp.bfloat16)
    grad_out_weight = dot_f32(merged, grad_branch, ((0,), (0,))).astype(jnp.bfloat16)
    grad_out_up = jnp.concatenate([grad_out_weight, grad_up], axis=1)
    grad_out_up, grad_merged = lax.optimization_barrier((grad_out_up, grad_merged))
    piece_out_up = scatter(grad_out_up)

    backs = []
    for g, (group, part) in enumerate(zip(groups, parts)):
        lo, hi = g * piece, (g + 1) * piece
        grads = grad_merged[:, lo:hi]
        if g == SPLITS - 1:
            for bit in bits[1:2]:
                blocks_down = halving_step(blocks_down, size, bit)
            grads, blocks_down = lax.optimization_barrier((grads, blocks_down))
        dq, *rest = attend_backward(images, place, valid, *group, part[1], grads)
        dk, dv = rest[0], rest[shards]
        for j in range(1, shards):
            dk = dk + shift(rest[j], shards, j).astype(jnp.float32)
            dv = dv + shift(rest[shards + j], shards, j).astype(jnp.float32)
        dk, dv = dk.astype(jnp.bfloat16), dv.astype(jnp.bfloat16)
        backs.append((dq, dk, dv))
    grad_mixed = jnp.concatenate(
        [back[part] for part in range(3) for back in backs], axis=1
    )
    grad_qkv = dot_f32(first, grad_mixed, ((0,), (0,))).astype(jnp.bfloat16)
    grad_first = dot_f32(grad_mixed, full_qkv, ((1,), (1,)))
    grad_tok_norm, grad_gain_one, grad_bias_one = pull_one(grad_first)
    grad_tokens = (grad_resid + grad_tok_norm).reshape(token_shape)

    def token_sum(values):
        return jnp.sum(values.astype(jnp.float32), axis=0)

    small_grads = jnp.stack(
        [
            grad_gain_one, grad_gain_two, grad_bias_one,
            token_sum(grad_mixed[:, :width]), token_sum(grad_mixed[:, 2 * width :]),
            token_sum(grad_branch), grad_bias_two, token_sum(grad_output),
        ],
        axis=1,
    )
    small_grads = jnp.concatenate([small_grads, token_sum(grad_upward).reshape(width, -1)], axis=1)
    small_grads = jnp.pad(small_grads, ((0, 0), (0, SMALL - small_grads.shape[1])))
    grad_qkvs = jnp.concatenate([grad_qkv, small_grads.astype(jnp.bfloat16)], axis=1)
    grad_qkvs, piece_out_up = lax.optimization_barrier((grad_qkvs, piece_out_up))
    for bit in bits[2:]:
        blocks_down = halving_step(blocks_down, size, bit)
    piece_down = blocks_down[0]
    piece_qkvs = scatter(grad_qkvs)

    output = residual + jnp.dot(activated, full_down, preferred_element_type=jnp.float32)
    out_tokens = (output + bias_down).astype(jnp.bfloat16).reshape(token_shape)

    def both(values):
        if shards == 2:
            return values.astype(jnp.float32) + shift(values, shards, 1).astype(jnp.float32)
        return lax.psum(values, "seq").astype(jnp.float32)

    total_down, total_out_up, total_qkvs = both(piece_down), both(piece_out_up), both(piece_qkvs)
    total_small = total_qkvs[:, 3 * width :]
    return (
        out_tokens,
        grad_tokens,
        total_qkvs[:, : 3 * width],
        total_out_up[:, :width],
        total_out_up[:, width:],
        total_down,
        total_small[:, :2],
        total_small[:, 2:8],
        total_small[:, 8 : 8 + ups].reshape(-1),
    )


def solution(mesh):
    return jax.shard_map(
        per_device,
        mesh=mesh,
        in_specs=(
            P("dp", "seq", None),
            P("dp", None),
            P("dp", None),
            P("dp", None),
            P("dp", None),
            P("dp", None),
            P("dp", None),
            P("dp"),
            P("dp"),
            P("dp", "seq", None),
        ),
        out_specs=(
            P("dp", "seq", None),
            P("dp", "seq", None),
            P("dp", None),
            P("dp", None),
            P("dp", None),
            P("dp", None),
            P("dp", None),
            P("dp", None),
            P("dp"),
        ),
        check_vma=False,
    )
```
